32 devices in a mesh: row: 8 (over y, x, core), col: 4 (over z).
Axes of the slice: x: 2, y: 2, z: 4, core: 2. Of those that a mesh axis runs over, the one named last changes fastest.
Arguments:
- operator: bfloat16 [36864, 36864], P('row', 'col'), may hold values from -0.046875 to 0.046875
- sketch_right: bfloat16 [36864, 384], P(('col', 'row')), may hold values from -6 to 6
- sketch_left: bfloat16 [36864, 576], P(('row', 'col')), may hold values from -6 to 6
Outputs:
- left_factor: bfloat16 [36864, 384], P('row')
- right_factor: bfloat16 [36864, 384], P(('col', 'row'))
The draws below stay inside these ranges and needn't reach their ends.
All inputs are finite; a program needn't handle non-finite values.
Results may differ from the reference program's by a relative error of at most 0.0015.
Values may be sent and summed in bfloat16 or wider, within the bound.
A program may use at most 192 MiB of HBM per device.

```python
import math
import jax
import jax.numpy as jnp
from jax import lax

N = 36864
R = 384
L = 576


def raised(entries, rng, source, target, shards_of, factor):
    owner, partner = [(jnp.arange(entries.shape[position]) // (entries.shape[position] // shards_of)).reshape([-1 if axis == position else 1 for axis in range(entries.ndim)]) for position in (source, target)]
    chosen = jax.random.permutation(rng, shards_of)[partner]
    strong = (owner == chosen) | (owner == (partner + shards_of // 2) % shards_of)
    return jnp.where(strong, factor * entries, entries)


def level_of(key, dims, shards, least, high):
    factor_of, own = 1.0, jax.random.fold_in(key, 6)
    for dim, parts in shards:
        heights = jnp.exp(jax.random.uniform(jax.random.fold_in(own, dim), (parts,), jnp.float32, least / len(shards), high / len(shards)))
        factor_of = factor_of * jnp.repeat(heights, dims[dim] // parts).reshape([-1 if axis == dim else 1 for axis in range(len(dims))])
    return factor_of


def gaussian(stream_key, dims, deviation, most, shards=(), kind=jnp.bfloat16):
    array = deviation * jax.random.normal(stream_key, dims, jnp.float32)
    if shards:
        array = array * level_of(stream_key, dims, shards, -0.22, 0.18)
    return jnp.clip(array, -most, most).astype(kind)


def heavy_noise(key, dims, spread, most, split, heavy, kind=jnp.bfloat16):
    drawn = spread * jax.random.normal(key, dims, jnp.float32)
    if split:
        drawn = drawn * level_of(key, dims, split, -0.22, 0.18)
    return jnp.clip(raised(drawn, jax.random.fold_in(key, 3), *heavy), -most, most).astype(kind)


def setup_inputs(seed: int = 0) -> dict:
    key_of = jax.random.split(jax.random.key(seed), 4)
    operator = heavy_noise(key_of[0], (N, N), N ** -0.5, 0.046875, ((0, 8), (1, 4)), (0, 1, 8, 2.0))
    sketch_right = gaussian(key_of[1], (N, R), 1.0, 6.0, ((0, 32),))
    sketch_left = gaussian(key_of[2], (N, L), 1.0, 6.0, ((0, 32),))
    return dict(operator=operator, sketch_right=sketch_right, sketch_left=sketch_left)


def transposed_product(wide, sketch):
    contract = (((0,), (0,)), ((), ()))
    high_part = wide.astype(jnp.bfloat16)
    rest = wide - lax.optimization_barrier(high_part).astype(jnp.float32)
    middle_part = rest.astype(jnp.bfloat16)
    low_part = (rest - lax.optimization_barrier(middle_part).astype(jnp.float32)).astype(jnp.bfloat16)
    total = lax.dot_general(high_part.astype(jnp.float32), sketch.astype(jnp.float32), contract, preferred_element_type=jnp.float32)
    total = total + lax.dot_general(middle_part.astype(jnp.float32), sketch.astype(jnp.float32), contract, preferred_element_type=jnp.float32)
    return total + lax.dot_general(low_part.astype(jnp.float32), sketch.astype(jnp.float32), contract, preferred_element_type=jnp.float32)

def reference(operator, sketch_right, sketch_left):
    image = jnp.dot(operator.astype(jnp.float32), sketch_right.astype(jnp.float32), preferred_element_type=jnp.float32)
    wide = lax.dot_general(operator.astype(jnp.float32), sketch_left.astype(jnp.float32), (((0,), (0,)), ((), ())), preferred_element_type=jnp.float32)
    core = transposed_product(wide, sketch_right)
    gram = jnp.dot(core.T, core, precision=lax.Precision.HIGHEST)
    lower = jnp.linalg.cholesky(gram)
    identity = jnp.eye(gram.shape[0], dtype=jnp.float32)
    inverse = jax.scipy.linalg.solve_triangular(lower, identity, lower=True).T
    ortho = jnp.dot(core, inverse, precision=lax.Precision.HIGHEST)
    factor = math.sqrt(N * L)
    left_factor = (factor * jnp.dot(image, inverse, precision=lax.Precision.HIGHEST)).astype(jnp.bfloat16)
    right_factor = jnp.dot(wide, ortho, precision=lax.Precision.HIGHEST).astype(jnp.bfloat16)
    return (left_factor, right_factor)
```

```python
import math

import jax
import jax.numpy as jnp
from jax import lax
from jax.sharding import PartitionSpec as P

HIGHEST = lax.Precision.HIGHEST


def bits_of(size):
    return [1 << i for i in range(size.bit_length() - 1)]


def exchange(x, axis, size, bit):
    return lax.ppermute(x, axis, [(i, i ^ bit) for i in range(size)])


def has(axis, bit):
    return (lax.axis_index(axis) // bit) % 2


def split(x, axis, bit):
    mine = has(axis, bit)
    kept = lax.dynamic_index_in_dim(x, mine, 0, keepdims=False)
    sent = lax.dynamic_index_in_dim(x, 1 - mine, 0, keepdims=False)
    return kept, sent


def join(mine, other, axis, bit, dim):
    first = has(axis, bit) == 0
    return jnp.stack(
        [jnp.where(first, mine, other), jnp.where(first, other, mine)], axis=dim
    )


def gather_order(block, axis, size, order):
    rank = block.ndim
    done = []
    for bit in order:
        place = sum(1 for b in done if b > bit)
        block = join(block, exchange(block, axis, size, bit), axis, bit, place)
        done.append(bit)
    return block.reshape((-1,) + block.shape[block.ndim - rank:])


def gather_rows(x, axis, size):
    bits = bits_of(size)
    core, rest = bits[0], bits[1:]
    half = x.shape[0] // 2
    parts = [
        gather_order(x[:half], axis, size, rest),
        gather_order(x[half:], axis, size, rest[::-1]),
    ]
    parts = [join(p, exchange(p, axis, size, core), axis, core, 1) for p in parts]
    both = jnp.concatenate(parts, axis=2)
    return both.reshape(size * x.shape[0], x.shape[1])


def reduce_order(x, axis, size, order):
    left = sorted(order, reverse=True)
    for bit in order:
        x = jnp.moveaxis(x, left.index(bit), 0)
        left.remove(bit)
        kept, sent = split(x, axis, bit)
        x = kept + exchange(sent, axis, size, bit)
    return x


def column_pieces(x, axis, size):
    core = bits_of(size)[0]
    high, width = x.shape[0] // 2, x.shape[1] // size
    mine = has(axis, core)

    def pieces(top, side):
        return jnp.stack([
            lax.dynamic_slice(x, (top, (2 * j + side) * width), (high, width))
            for j in range(size // 2)
        ])

    kept = [pieces(i * high, mine) for i in range(2)]
    return kept, [pieces(i * high, 1 - mine) for i in range(2)]


def total_of(x, sizes):
    (row, rows), (col, cols) = sizes
    shape = x.shape
    bits = bits_of(rows)
    y = x.reshape((2,) * len(bits) + (shape[0] // rows, shape[1]))
    y = reduce_order(y, row, rows, bits)
    for bit in bits_of(cols):
        y = y + exchange(y, col, cols, bit)
    y = gather_order(y, row, rows, bits[::-1])
    return y.reshape(shape)


def left_product(sketch, image):
    contract = (((0,), (0,)), ((), ()))
    high_part = image.astype(jnp.bfloat16)
    rest = image - lax.optimization_barrier(high_part).astype(jnp.float32)
    middle_part = rest.astype(jnp.bfloat16)
    low_part = (rest - lax.optimization_barrier(middle_part).astype(jnp.float32)).astype(
        jnp.bfloat16
    )
    total = lax.dot_general(sketch, high_part, contract, preferred_element_type=jnp.float32)
    total = total + lax.dot_general(
        sketch, middle_part, contract, preferred_element_type=jnp.float32
    )
    return total + lax.dot_general(sketch, low_part, contract, preferred_element_type=jnp.float32)


def dot(a, b):
    return jnp.dot(a, b, precision=HIGHEST)


def inverse_factor(gram, tie, block=128):
    n = gram.shape[0]
    if n <= block:
        gram = tie(gram)
        lower = jnp.linalg.cholesky(gram)
        return jax.scipy.linalg.solve_triangular(
            lower, jnp.eye(n, dtype=gram.dtype), lower=True
        )
    head = inverse_factor(gram[:block, :block], lambda g: g, block)
    below = dot(gram[block:, :block], head.T)
    tail = inverse_factor(gram[block:, block:] - dot(below, below.T), tie, block)
    corner = -dot(tail, dot(below, head))
    top = jnp.concatenate([head, jnp.zeros((block, n - block), gram.dtype)], axis=1)
    return jnp.concatenate([top, jnp.concatenate([corner, tail], axis=1)], axis=0)


def solution(mesh):
    rows, cols = mesh.shape["row"], mesh.shape["col"]

    def on_device(operator, sketch_right, sketch_left):
        factor = math.sqrt(operator.shape[0] * rows * sketch_left.shape[1])
        left_rows = lax.all_gather(sketch_left, "col", axis=0, tiled=True)
        right_rows = gather_rows(sketch_right, "row", rows)
        image = jnp.dot(operator, right_rows, preferred_element_type=jnp.float32)
        image_piece = lax.psum_scatter(image, "col", scatter_dimension=0, tiled=True)
        core_term = left_product(left_rows, image)
        core_term, left_rows = lax.optimization_barrier((core_term, left_rows))
        core = total_of(core_term, (("row", rows), ("col", cols)))
        contract = (((0,), (0,)), ((), ()))
        wide = lax.dot_general(left_rows, operator, contract, preferred_element_type=jnp.float32)
        kept, sent = column_pieces(wide, "row", rows)
        core, sent = lax.optimization_barrier((core, sent))
        rest = bits_of(rows)[1:]
        orders = (rest, rest[::-1])
        halves = []
        for mine, other, order in zip(kept, sent, orders):
            part = mine + exchange(other, "row", rows, 1)
            part = part.reshape((2,) * len(rest) + part.shape[1:])
            place = sorted(order, reverse=True).index(order[0])
            halves.append(split(jnp.moveaxis(part, place, 0), "row", order[0]))

        def tie(gram):
            gram, outgoing = lax.optimization_barrier((gram, [h[1] for h in halves]))
            halves[:] = [
                reduce_order(
                    h[0] + exchange(out, "row", rows, order[0]), "row", rows, order[1:]
                )
                for h, out, order in zip(halves, outgoing, orders)
            ]
            return gram

        inverse = inverse_factor(dot(core.T, core), tie).T
        wide_piece = jnp.concatenate(halves, axis=0)
        left_piece = (factor * dot(image_piece, inverse)).astype(jnp.bfloat16)
        left_factor = lax.all_gather(left_piece, "col", axis=0, tiled=True)
        ortho = dot(core, inverse)
        right_factor = dot(wide_piece.T, ortho).astype(jnp.bfloat16)
        return (left_factor, right_factor)

    in_specs = (P("row", "col"), P(("col", "row"), None), P(("row", "col"), None))
    out_specs = (P("row", None), P(("col", "row"), None))
    return jax.shard_map(
        on_device, mesh=mesh, in_specs=in_specs, out_specs=out_specs, check_vma=False
    )
```
